32 devices in a mesh: space: 16 (over z, x, core), mem: 2 (over y).
Axes of the slice: x: 2, y: 2, z: 4, core: 2. Of those that a mesh axis runs over, the one named last changes fastest.
Arguments:
- ensemble: bfloat16 [8, 32, 512, 1536], P('mem', None, 'space'), may hold values from -12 to 12
- vector: bfloat16 [32, 512, 1536], P(None, 'space'), may hold values from -6 to 6
- modes: float32 [16, 32], replicated, may hold values from -1 to 1
- legendre: bfloat16 [512, 512, 256], P('space'), may hold values from -0.25 to 0.25
- spectrum: float32 [512, 256], P('space'), may hold values from 0.1 to 1
- truncation: int32 [1], replicated, may hold values from 543 to 702
Outputs:
- covariance_apply: bfloat16 [32, 512, 1536], P(None, 'space')
The draws below stay inside these ranges and needn't reach their ends.
All inputs are finite; a program needn't handle non-finite values.
Results may differ from the reference program's by a relative error of at most 0.014.
Values may be sent and summed in bfloat16 or wider, within the bound.
A program may use at most 128 MiB of HBM per device.

```python
import math
import jax
import jax.numpy as jnp
from jax import lax

NLEV = 32
NMODE = 16
NLON = 1536
NLAT = 512
M = 512
NDEG = 256
MEMBERS = 8


def block_scale(key, shape, shards, low, largest):
    loudness = 1.0
    for axis_at, parts in shards:
        steps = jax.random.uniform(jax.random.fold_in(jax.random.fold_in(key, 6), axis_at), (parts,), jnp.float32, low / len(shards), largest / len(shards))
        loudness = loudness * jnp.repeat(jnp.exp(steps), shape[axis_at] // parts).reshape((-1,) + (1,) * (len(shape) - 1 - axis_at))
    return loudness


def scatter_about(own_key, shape, deviation, bound, shards=(), kind=jnp.bfloat16):
    loudness = block_scale(own_key, shape, shards, -0.22, 0.18) if shards else 1.0
    values = jax.random.normal(own_key, shape, jnp.float32) * deviation * loudness
    return jnp.minimum(jnp.maximum(values, -bound), bound).astype(kind)


def setup_inputs(seed: int = 0) -> dict:
    key_list = jax.random.split(jax.random.key(seed), 7)
    return {
        "ensemble": scatter_about(key_list[0], (MEMBERS, NLEV, NLAT, NLON), 2.0, 12.0, ((0, 2), (2, 16))),
        "vector": scatter_about(key_list[1], (NLEV, NLAT, NLON), 1.0, 6.0, ((1, 16),)),
        "modes": scatter_about(key_list[2], (NMODE, NLEV), NLEV ** -0.5, 1.0, (), jnp.float32),
        "legendre": scatter_about(key_list[3], (M, NLAT, NDEG), NLAT ** -0.5, 0.25, ((0, 16),)),
        "spectrum": jnp.clip(jnp.exp(math.log(1.0) - 2.3025851 * jax.random.uniform(key_list[4], (M, NDEG), jnp.float32) ** block_scale(key_list[4], (M, NDEG), ((0, 16),), -0.2, 0.2)), 0.1, 1.0),
        "truncation": jax.random.randint(key_list[5], (1,), M - 1 + NDEG // 8, M - 1 + 3 * NDEG // 4).astype(jnp.int32),
    }


def fourier_table(length, wave_count):
    points = jnp.arange(length, dtype=jnp.int32)
    orders = jnp.arange(wave_count, dtype=jnp.int32)
    phases = points[:, None] * orders[None, :] % length
    angles = phases.astype(jnp.float32) * (2.0 * math.pi / length)
    amplitude = math.sqrt(2.0 / length)
    stacked = jnp.stack([jnp.cos(angles), -jnp.sin(angles)], axis=-1) * amplitude
    return stacked.reshape(length, 2 * wave_count).astype(jnp.bfloat16)

def reference(ensemble, vector, modes, legendre, spectrum, truncation):
    fourier = fourier_table(NLON, M)
    wavenumber = jnp.arange(M, dtype=jnp.int32)[:, None] + jnp.arange(NDEG, dtype=jnp.int32)[None, :]
    factor = jnp.where(wavenumber <= truncation[0], spectrum, jnp.zeros_like(spectrum))
    legendre_wide = legendre.astype(jnp.float32)
    vector_wide = vector.astype(jnp.float32)
    highest = lax.Precision.HIGHEST

    def member(running, anomaly):
        product = anomaly.astype(jnp.float32) * vector_wide
        projected = jnp.einsum('jl,lac->jac', modes, product, precision=highest).astype(jnp.bfloat16)
        zonal_parts = jnp.dot(projected.reshape(NMODE * NLAT, NLON), fourier, preferred_element_type=jnp.float32)
        zonal_parts = lax.optimization_barrier(zonal_parts.astype(jnp.bfloat16))
        zonal_wide = zonal_parts.astype(jnp.float32).reshape(NMODE, NLAT, M, 2)
        harmonic = jnp.einsum('jamr,man->jmrn', zonal_wide, legendre_wide)
        weighted = lax.optimization_barrier((harmonic * factor[None, :, None, :]).astype(jnp.bfloat16))
        weighted_wide = weighted.astype(jnp.float32)
        synthesis = jnp.einsum('jmrn,man->jamr', weighted_wide, legendre_wide).astype(jnp.bfloat16)
        spread = jnp.dot(synthesis.reshape(NMODE * NLAT, 2 * M), fourier.T, preferred_element_type=jnp.float32)
        spread = spread.reshape(NMODE, NLAT, NLON)
        lifted = jnp.einsum('jl,jac->lac', modes, spread, precision=highest)
        return (running + anomaly.astype(jnp.float32) * lifted, None)
    start = jnp.zeros((NLEV, NLAT, NLON), jnp.float32)
    summed, _ = lax.scan(member, start, ensemble)
    return (summed / (MEMBERS - 1)).astype(jnp.bfloat16)
```

```python
import math

import jax
import jax.numpy as jnp
from jax import lax
from jax.experimental import pallas as pl
from jax.experimental.pallas import tpu as pltpu
from jax.sharding import PartitionSpec as P

NMODE = 16
NLON = 1536
M = 512
NDEG = 256


def fourier_table(length, wave_count):
    points = jnp.arange(length, dtype=jnp.int32)
    orders = jnp.arange(wave_count, dtype=jnp.int32)
    phases = points[:, None] * orders[None, :] % length
    angles = phases.astype(jnp.float32) * (2.0 * math.pi / length)
    amplitude = math.sqrt(2.0 / length)
    stacked = jnp.stack([jnp.cos(angles), -jnp.sin(angles)], axis=-1) * amplitude
    return stacked.reshape(length, 2 * wave_count).astype(jnp.bfloat16)


def plain_path(ensemble, vector, modes, legendre, spectrum, truncation):
    members = ensemble.shape[0]
    lat_rows = ensemble.shape[2]
    own_waves = legendre.shape[0]
    sources = lax.axis_size("space")
    total_members = members * lax.axis_size("mem")
    highest = lax.Precision.HIGHEST
    fourier = fourier_table(NLON, M)
    product = ensemble.astype(jnp.float32) * vector.astype(jnp.float32)[None]
    projected = jnp.einsum("jl,klac->kjac", modes, product, precision=highest).astype(jnp.bfloat16)
    fields = members * NMODE
    columns = fields * lat_rows
    zonal_parts = lax.dot_general(
        fourier,
        projected.reshape(columns, NLON),
        (((0,), (1,)), ((), ())),
        preferred_element_type=jnp.float32,
    )
    zonal_parts = zonal_parts.astype(jnp.bfloat16).reshape(1, 2 * M, columns)
    first_wave = lax.axis_index("space") * own_waves
    wavenumber = (
        first_wave
        + jnp.arange(own_waves, dtype=jnp.int32)[:, None]
        + jnp.arange(NDEG, dtype=jnp.int32)[None, :]
    )
    factor = jnp.where(wavenumber <= truncation[0], spectrum, jnp.zeros_like(spectrum))
    arrived = lax.all_to_all(zonal_parts, "space", split_axis=1, concat_axis=0, tiled=True)
    arrived = arrived.reshape(sources, own_waves, 2, fields, lat_rows)
    legendre_view = legendre.reshape(own_waves, sources, lat_rows, NDEG)
    harmonic = jnp.einsum(
        "smrfa,msan->mrfn", arrived, legendre_view, preferred_element_type=jnp.float32
    )
    weighted = (harmonic * factor[:, None, None, :]).astype(jnp.bfloat16)
    synthesis = jnp.einsum(
        "mrfn,msan->smrfa", weighted, legendre_view, preferred_element_type=jnp.float32
    )
    synthesis = synthesis.astype(jnp.bfloat16).reshape(sources, 2 * own_waves, columns)
    returned = lax.all_to_all(synthesis, "space", split_axis=0, concat_axis=1, tiled=True)
    spread = lax.dot_general(
        returned.reshape(2 * M, columns),
        fourier,
        (((0,), (1,)), ((), ())),
        preferred_element_type=jnp.float32,
    )
    spread = spread.reshape(members, NMODE, lat_rows, NLON)
    lifted = jnp.einsum("jl,kjac->klac", modes, spread, precision=highest)
    partial_value = jnp.sum(ensemble.astype(jnp.float32) * lifted, axis=0)
    summed = lax.psum(partial_value.astype(jnp.bfloat16), "mem").astype(jnp.float32)
    return (summed / (total_members - 1)).astype(jnp.bfloat16)


F32 = jnp.float32
BF16 = jnp.bfloat16
TILE = 16
LANES = 128
BIG = 63 * 1024 * 1024


def nt(a, b):
    return lax.dot_general(a, b, (((1,), (1,)), ((), ())), preferred_element_type=F32)


def nn(a, b):
    return lax.dot_general(a, b, (((1,), (0,)), ((), ())), preferred_element_type=F32)


def fourier_factors():
    row = jnp.arange(2 * M, dtype=jnp.int32)[:, None]
    lane = jnp.arange(LANES, dtype=jnp.int32)[None, :]
    wave, part = row // 2, row % 2
    step = 2.0 * math.pi / NLON
    high = ((wave * LANES * lane + part * (NLON // 4)) % NLON).astype(F32) * step
    low = (wave * lane % NLON).astype(F32) * step
    amplitude = math.sqrt(2.0 / NLON)
    return jnp.stack([jnp.cos(high) * amplitude, jnp.sin(high) * amplitude, jnp.cos(low), jnp.sin(low)])


def build_table(factors_ref, table_ref):
    rows = 128

    @pl.loop(0, 2 * M // rows)
    def _(i):
        own = pl.ds(pl.multiple_of(i * rows, rows), rows)
        low_cos, low_sin = factors_ref[2, own, :], factors_ref[3, own, :]
        for high in range(NLON // LANES):
            high_cos = factors_ref[0, own, high : high + 1]
            high_sin = factors_ref[1, own, high : high + 1]
            value = high_cos * low_cos - high_sin * low_sin
            table_ref[own, high * LANES : (high + 1) * LANES] = value.astype(BF16)


def greet(axis, count):
    me = lax.axis_index(axis)
    barrier = pltpu.get_barrier_semaphore()

    @pl.loop(1, count)
    def _(i):
        pl.semaphore_signal(barrier, inc=1, device_id={axis: lax.rem(me + i, count)}, device_id_type=pl.DeviceIdType.MESH)

    pl.semaphore_wait(barrier, count - 1)


def send(axis, src, dst, send_sem, recv_sem, target):
    return pltpu.make_async_remote_copy(
        src_ref=src,
        dst_ref=dst,
        send_sem=send_sem,
        recv_sem=recv_sem,
        device_id={axis: target},
        device_id_type=pl.DeviceIdType.MESH,
    )


def forward_kernel(sources, ens_hbm, vec_hbm, weight_ref, factors_ref, out_ref,
                   ens, vec, table, fields, turn, packed, load_sem, own_sem, send_sem, recv_sem):
    me = lax.axis_index("space")
    members = ens.shape[0]
    groups = ens.shape[2] // TILE
    share = 2 * M // sources
    width = 512
    loads = [pltpu.make_async_copy(vec_hbm, vec, load_sem.at[members])]
    loads += [pltpu.make_async_copy(ens_hbm.at[k], ens.at[k], load_sem.at[k]) for k in range(members)]
    for load in loads:
        load.start()
    build_table(factors_ref, table)
    greet("space", sources)
    loads[0].wait()
    levels = ens.shape[1]
    for k in range(members):
        loads[k + 1].wait()

        @pl.loop(0, groups * (NLON // width))
        def _(i):
            g, c = i // (NLON // width), lax.rem(i, NLON // width)
            rows = pl.ds(pl.multiple_of(g * TILE, TILE), TILE)
            columns = pl.ds(pl.multiple_of(c * width, width), width)
            product = ens[k, :, rows, columns] * vec[:, rows, columns]
            result = nn(weight_ref[...], product.reshape(levels * TILE, width))
            fields[:, g, k, :, columns] = result.astype(BF16).reshape(TILE, NMODE, width)

    per_block = 4
    lat_width = groups * members * NMODE

    @pl.loop(0, sources // per_block)
    def _(block):
        targets = [lax.rem(me + block * per_block + i + 1, sources) for i in range(per_block)]
        lhs = jnp.concatenate([table[pl.ds(pl.multiple_of(d * share, share), share), :] for d in targets], axis=0)
        for pair in range(TILE // 2):
            rhs = fields[2 * pair : 2 * pair + 2].reshape(2 * lat_width, NLON)
            result = nt(lhs, rhs)
            turn[:, 2 * pair, :] = result[:, :LANES]
            turn[:, 2 * pair + 1, :] = result[:, LANES:]
        for i in range(per_block):
            slot = block * per_block + i
            packed[slot] = turn[i * share : (i + 1) * share].astype(BF16)
        for i in range(per_block):
            slot = block * per_block + i

            @pl.when(slot < sources - 1)
            def _():
                send("space", packed.at[slot], out_ref.at[me], send_sem.at[slot], recv_sem.at[me], targets[i]).start()

    own = pltpu.make_async_copy(packed.at[sources - 1], out_ref.at[me], own_sem.at[0])
    own.start()

    @pl.loop(0, sources - 1)
    def _(slot):
        other = lax.rem(me + slot + 1, sources)
        send("space", packed.at[slot], out_ref.at[other], send_sem.at[slot], recv_sem.at[other], other).wait()

    own.wait()


def spectral_kernel(sources, arrived, legendre, factor, out_ref,
                    packed, own_sem, send_sem, recv_sem):
    me = lax.axis_index("space")
    own_waves = legendre.shape[0]
    lat_rows = 2 * TILE
    greet("space", sources)
    half = LANES // 2

    @pl.loop(0, own_waves)
    def _(m):
        table = legendre[m].reshape(sources, 2, TILE, NDEG)
        halves = [table[:, h].reshape(sources * TILE, NDEG) for h in range(2)]
        stacked = [arrived[:, 2 * m + r].reshape(sources * TILE, LANES).T for r in range(2)]
        harmonic = 0.0
        for h in range(2):
            lhs = jnp.concatenate([z[h * half : (h + 1) * half] for z in stacked], axis=0)
            harmonic = harmonic + nn(lhs, halves[h])
        weighted = (harmonic * factor[pl.ds(m, 1), :]).astype(BF16)
        zero = jnp.zeros((half, NDEG), BF16)
        low = jnp.concatenate([weighted[:half], zero, weighted[half:], zero], axis=0)
        high = jnp.concatenate([zero, weighted[:half], zero, weighted[half:]], axis=0)
        synthesis = (nt(halves[0], low) + nt(halves[1], high)).astype(BF16)
        for r in range(2):
            block = synthesis[:, r * LANES : (r + 1) * LANES]
            packed[:, 2 * m + r] = block.reshape(sources, TILE, LANES)

    @pl.loop(1, sources)
    def _(i):
        other = lax.rem(me + i, sources)
        send("space", packed.at[other], out_ref.at[me], send_sem.at[i], recv_sem.at[me], other).start()

    own = pltpu.make_async_copy(packed.at[me], out_ref.at[me], own_sem.at[0])
    own.start()

    @pl.loop(1, sources)
    def _(i):
        other = lax.rem(me + i, sources)
        send("space", packed.at[other], out_ref.at[other], send_sem.at[i], recv_sem.at[other], other).wait()

    own.wait()


def inverse_kernel(returned, ens_hbm, lift_ref, factors_ref, out_ref,
                   ens, table, turn, fields, mine, theirs, load_sem, send_sem, recv_sem):
    me = lax.axis_index("mem")
    other = 1 - me
    members, levels, lat_rows = ens.shape[:3]
    groups = lat_rows // TILE
    width = 512
    pieces = NLON // width
    load = pltpu.make_async_copy(ens_hbm, ens, load_sem.at[0])
    load.start()
    build_table(factors_ref, table)
    greet("mem", 2)
    sources, share = returned.shape[:2]

    @pl.loop(0, sources)
    def _(s):
        turn[pl.ds(pl.multiple_of(s * share, share), share)] = returned[s].astype(F32)

    for pair in range(TILE // 2):
        lhs = jnp.concatenate([turn[:, 2 * pair + i, :].astype(BF16).T for i in range(2)], axis=0)

        @pl.loop(0, pieces)
        def _(c):
            columns = pl.ds(pl.multiple_of(c * width, width), width)
            result = nn(lhs, table[:, columns]).astype(BF16).reshape(2, groups, members, NMODE, width)
            for i in range(2):
                fields[:, :, 2 * pair + i, :, columns] = result[i]

    load.wait()

    @pl.loop(0, groups * pieces)
    def _(i):
        g, c = i // pieces, lax.rem(i, pieces)
        rows = pl.ds(pl.multiple_of(g * TILE, TILE), TILE)
        columns = pl.ds(pl.multiple_of(c * width, width), width)
        total = 0.0
        for k in range(members):
            lifted = nn(lift_ref[...], fields[g, k, :, :, columns].reshape(TILE * NMODE, width))
            anomaly = ens[k, :, rows, columns].reshape(levels * TILE, width)
            total = total + lifted * anomaly.astype(F32)
        mine[i] = total.astype(BF16)
        send("mem", mine.at[i], theirs.at[i], send_sem.at[i], recv_sem.at[i], other).start()

    scale = 1.0 / (2 * members - 1)

    @pl.loop(0, groups * pieces)
    def _(i):
        g, c = i // pieces, lax.rem(i, pieces)
        rows = pl.ds(pl.multiple_of(g * TILE, TILE), TILE)
        columns = pl.ds(pl.multiple_of(c * width, width), width)
        send("mem", mine.at[i], theirs.at[i], send_sem.at[i], recv_sem.at[i], other).wait()
        summed = (mine[i].astype(F32) + theirs[i].astype(F32)) * scale
        out_ref[:, rows, columns] = summed.astype(BF16).reshape(levels, TILE, width)


def params(number):
    return pltpu.CompilerParams(collective_id=number, has_side_effects=True, vmem_limit_bytes=BIG)


def kernel_path(ensemble, vector, modes, legendre, spectrum, truncation):
    members, levels, lat_rows, _ = ensemble.shape
    own_waves = legendre.shape[0]
    sources = lax.axis_size("space")
    share = 2 * own_waves
    factors = fourier_factors()
    same = jnp.eye(TILE, dtype=F32)
    weight = same[:, None, None, :] * modes[None, :, :, None]
    weight = weight.reshape(TILE * NMODE, levels * TILE).astype(BF16)
    lift = same[None, :, :, None] * modes.T[:, None, None, :]
    lift = lift.reshape(levels * TILE, TILE * NMODE).astype(BF16)
    wavenumber = (
        lax.axis_index("space") * own_waves
        + jnp.arange(own_waves, dtype=jnp.int32)[:, None]
        + jnp.arange(NDEG, dtype=jnp.int32)[None, :]
    )
    factor = jnp.where(wavenumber <= truncation[0], spectrum, jnp.zeros_like(spectrum))
    any_space = pl.BlockSpec(memory_space=pl.ANY)
    vmem = pl.BlockSpec(memory_space=pltpu.VMEM)
    exchanged = jax.ShapeDtypeStruct((sources, share, TILE, LANES), BF16)
    groups = lat_rows // TILE
    width = 512
    pieces = groups * (NLON // width)
    dma = pltpu.SemaphoreType.DMA
    arrived = pl.pallas_call(
        lambda *refs: forward_kernel(sources, *refs),
        out_shape=exchanged,
        in_specs=[any_space, any_space, vmem, vmem],
        out_specs=any_space,
        scratch_shapes=[
            pltpu.VMEM(ensemble.shape, BF16),
            pltpu.VMEM(vector.shape, BF16),
            pltpu.VMEM((2 * M, NLON), BF16),
            pltpu.VMEM((TILE, groups, members, NMODE, NLON), BF16),
            pltpu.VMEM((4 * share, TILE, LANES), F32),
            pltpu.VMEM((sources, share, TILE, LANES), BF16),
            dma((members + 1,)),
            dma((1,)),
            dma((sources,)),
            dma((sources,)),
        ],
        compiler_params=params(0),
        name="forward",
    )(ensemble, vector, weight, factors)
    returned = pl.pallas_call(
        lambda *refs: spectral_kernel(sources, *refs),
        out_shape=exchanged,
        in_specs=[vmem, vmem, vmem],
        out_specs=any_space,
        scratch_shapes=[
            pltpu.VMEM((sources, share, TILE, LANES), BF16),
            dma((1,)),
            dma((sources,)),
            dma((sources,)),
        ],
        compiler_params=params(1),
        name="spectral",
    )(arrived, legendre, factor)
    return pl.pallas_call(
        inverse_kernel,
        out_shape=jax.ShapeDtypeStruct(vector.shape, BF16),
        in_specs=[vmem, any_space, vmem, vmem],
        out_specs=vmem,
        scratch_shapes=[
            pltpu.VMEM(ensemble.shape, BF16),
            pltpu.VMEM((2 * M, NLON), BF16),
            pltpu.VMEM((2 * M, TILE, LANES), F32),
            pltpu.VMEM((groups, members, TILE, NMODE, NLON), BF16),
            pltpu.VMEM((pieces, levels * TILE, width), BF16),
            pltpu.VMEM((pieces, levels * TILE, width), BF16),
            dma((1,)),
            dma((pieces,)),
            dma((pieces,)),
        ],
        compiler_params=params(2),
        name="inverse",
    )(returned, ensemble, lift, factors)


def on_device(ensemble, vector, modes, legendre, spectrum, truncation):
    fits = (
        lax.axis_size("mem") == 2
        and lax.axis_size("space") % 4 == 0
        and ensemble.shape[2] == 2 * TILE
        and 2 * ensemble.shape[0] * NMODE == LANES
        and modes.shape[1] == 32
    )
    path = kernel_path if fits else plain_path
    return path(ensemble, vector, modes, legendre, spectrum, truncation)


def solution(mesh):
    placed = (
        P("mem", None, "space", None),
        P(None, "space", None),
        P(),
        P("space", None, None),
        P("space", None),
        P(),
    )
    return jax.shard_map(
        on_device, mesh=mesh, in_specs=placed, out_specs=P(None, "space", None), check_vma=False
    )
```

```python
import math

import jax
import jax.numpy as jnp
from jax import lax
from jax.experimental import pallas as pl
from jax.experimental.pallas import tpu as pltpu
from jax.sharding import PartitionSpec as P

NMODE = 16
NLON = 1536
M = 512
NDEG = 256


def fourier_table(length, wave_count):
    points = jnp.arange(length, dtype=jnp.int32)
    orders = jnp.arange(wave_count, dtype=jnp.int32)
    phases = points[:, None] * orders[None, :] % length
    angles = phases.astype(jnp.float32) * (2.0 * math.pi / length)
    amplitude = math.sqrt(2.0 / length)
    stacked = jnp.stack([jnp.cos(angles), -jnp.sin(angles)], axis=-1) * amplitude
    return stacked.reshape(length, 2 * wave_count).astype(jnp.bfloat16)


def plain_path(ensemble, vector, modes, legendre, spectrum, truncation):
    members = ensemble.shape[0]
    lat_rows = ensemble.shape[2]
    own_waves = legendre.shape[0]
    sources = lax.axis_size("space")
    total_members = members * lax.axis_size("mem")
    highest = lax.Precision.HIGHEST
    fourier = fourier_table(NLON, M)
    product = ensemble.astype(jnp.float32) * vector.astype(jnp.float32)[None]
    projected = jnp.einsum("jl,klac->kjac", modes, product, precision=highest).astype(jnp.bfloat16)
    fields = members * NMODE
    columns = fields * lat_rows
    zonal_parts = lax.dot_general(
        fourier,
        projected.reshape(columns, NLON),
        (((0,), (1,)), ((), ())),
        preferred_element_type=jnp.float32,
    )
    zonal_parts = zonal_parts.astype(jnp.bfloat16).reshape(1, 2 * M, columns)
    first_wave = lax.axis_index("space") * own_waves
    wavenumber = (
        first_wave
        + jnp.arange(own_waves, dtype=jnp.int32)[:, None]
        + jnp.arange(NDEG, dtype=jnp.int32)[None, :]
    )
    factor = jnp.where(wavenumber <= truncation[0], spectrum, jnp.zeros_like(spectrum))
    arrived = lax.all_to_all(zonal_parts, "space", split_axis=1, concat_axis=0, tiled=True)
    arrived = arrived.reshape(sources, own_waves, 2, fields, lat_rows)
    legendre_view = legendre.reshape(own_waves, sources, lat_rows, NDEG)
    harmonic = jnp.einsum(
        "smrfa,msan->mrfn", arrived, legendre_view, preferred_element_type=jnp.float32
    )
    weighted = (harmonic * factor[:, None, None, :]).astype(jnp.bfloat16)
    synthesis = jnp.einsum(
        "mrfn,msan->smrfa", weighted, legendre_view, preferred_element_type=jnp.float32
    )
    synthesis = synthesis.astype(jnp.bfloat16).reshape(sources, 2 * own_waves, columns)
    returned = lax.all_to_all(synthesis, "space", split_axis=0, concat_axis=1, tiled=True)
    spread = lax.dot_general(
        returned.reshape(2 * M, columns),
        fourier,
        (((0,), (1,)), ((), ())),
        preferred_element_type=jnp.float32,
    )
    spread = spread.reshape(members, NMODE, lat_rows, NLON)
    lifted = jnp.einsum("jl,kjac->klac", modes, spread, precision=highest)
    partial_value = jnp.sum(ensemble.astype(jnp.float32) * lifted, axis=0)
    summed = lax.psum(partial_value.astype(jnp.bfloat16), "mem").astype(jnp.float32)
    return (summed / (total_members - 1)).astype(jnp.bfloat16)


F32 = jnp.float32
BF16 = jnp.bfloat16
TILE = 16
LANES = 128
BIG = 63 * 1024 * 1024


def nt(a, b):
    return lax.dot_general(a, b, (((1,), (1,)), ((), ())), preferred_element_type=F32)


def nn(a, b):
    return lax.dot_general(a, b, (((1,), (0,)), ((), ())), preferred_element_type=F32)


def cosine(phase):
    phase = lax.rem(phase, NLON)
    offset = (jnp.abs(phase - NLON // 2) - NLON // 4).astype(F32)
    x = offset * (2.0 * math.pi / NLON)
    square = x * x
    value = 1.0
    for n in range(6, 0, -1):
        value = 1.0 - square * value * (1.0 / ((2 * n) * (2 * n + 1)))
    return x * value


def build_table(table_ref, waves_first):
    rows = 128
    quarter = NLON // 4
    amplitude = math.sqrt(2.0 / NLON)

    @pl.loop(0, 2 * M // rows)
    def _(i):
        start = pl.multiple_of(i * rows, rows)
        row = start + lax.broadcasted_iota(jnp.int32, (rows, LANES), 0)
        lane = lax.broadcasted_iota(jnp.int32, (rows, LANES), 1)
        wave, part = (lax.rem(row, M), row // M) if waves_first else (row // 2, lax.rem(row, 2))
        low_cos = cosine(wave * lane)
        low_sin = cosine(wave * lane + 3 * quarter)
        high = cosine(wave * LANES * lax.rem(lane, 64) + (part + 3 * (lane // 64)) * quarter) * amplitude
        for c in range(NLON // LANES):
            value = high[:, c : c + 1] * low_cos - high[:, 64 + c : 65 + c] * low_sin
            table_ref[pl.ds(start, rows), c * LANES : (c + 1) * LANES] = value.astype(BF16)


def greet(counts):
    barrier = pltpu.get_barrier_semaphore()
    for axis, count in counts:
        me = lax.axis_index(axis)
        for i in range(1, count):
            target = lax.rem(me + i, count)
            pl.semaphore_signal(barrier, inc=1, device_id={axis: target}, device_id_type=pl.DeviceIdType.MESH)
    pl.semaphore_wait(barrier, sum(count - 1 for _, count in counts))


def send(axis, src, dst, send_sem, recv_sem, target):
    return pltpu.make_async_remote_copy(
        src_ref=src,
        dst_ref=dst,
        send_sem=send_sem,
        recv_sem=recv_sem,
        device_id={axis: target},
        device_id_type=pl.DeviceIdType.MESH,
    )


def spread_modes(modes_ref, levels, across):
    tiled = jnp.concatenate([modes_ref[...]] * TILE, axis=0)
    long, short = levels * TILE, TILE * NMODE
    if across:
        pick = (lax.broadcasted_iota(jnp.int32, (levels, long), 1) // TILE) == lax.broadcasted_iota(jnp.int32, (levels, long), 0)
        value = nn(tiled, jnp.where(pick, 1.0, 0.0).astype(BF16))
        shape, long_at = (short, long), 1
    else:
        pick = (lax.broadcasted_iota(jnp.int32, (long, levels), 0) // TILE) == lax.broadcasted_iota(jnp.int32, (long, levels), 1)
        value = nt(jnp.where(pick, 1.0, 0.0).astype(BF16), tiled)
        shape, long_at = (long, short), 0
    agree = (lax.broadcasted_iota(jnp.int32, shape, long_at) % TILE) == (lax.broadcasted_iota(jnp.int32, shape, 1 - long_at) // NMODE)
    return jnp.where(agree, value, 0.0).astype(BF16)


ROW = 4
STEPS = (2, 1, 3, 0)


class Exchange:
    def __init__(self, sources, sources_at, landing_at, own_sem, send_sem, recv_sem):
        self.count = sources // ROW
        self.me = lax.axis_index("space")
        self.row, self.column = self.me // ROW, lax.rem(self.me, ROW)
        self.sources_at, self.landing_at = sources_at, landing_at
        self.own_sem, self.send_sem, self.recv_sem = own_sem, send_sem, recv_sem

    def device(self, step, i):
        return lax.rem(self.row + step + self.count, self.count) * ROW + lax.rem(self.column + i + ROW, ROW)

    def piece(self, step, i, part, source):
        at = step * ROW + i
        return send("space", self.sources_at(step, i, part), self.landing_at(source, part),
                    self.send_sem.at[part, at], self.recv_sem.at[part, at], self.device(step, i))

    def own(self, part):
        return pltpu.make_async_copy(self.sources_at(0, 0, part), self.landing_at(self.me, part), self.own_sem.at[part])

    def start(self, step, part):
        for i in range(ROW):
            if step == 0 and i == 0:
                self.own(part).start()
            else:
                self.piece(step, i, part, self.me).start()

    def finish(self, part):
        for step in STEPS:
            for i in range(ROW):
                if step == 0 and i == 0:
                    self.own(part).wait()
                else:
                    self.piece(step, i, part, self.device(-step, -i)).wait()


def forward_kernel(sources, ens_hbm, vec_hbm, modes_ref, out_ref,
                   weight_ref, ens, vec, table, fields, turn, packed, load_sem, *sems):
    me = lax.axis_index("space")
    members = ens.shape[0]
    groups = ens.shape[2] // TILE
    share = 2 * M // sources
    width = 512
    loads = [pltpu.make_async_copy(vec_hbm, vec, load_sem.at[members])]
    loads += [pltpu.make_async_copy(ens_hbm.at[k], ens.at[k], load_sem.at[k]) for k in range(members)]
    for load in loads:
        load.start()
    levels = ens.shape[1]
    weight_ref[...] = spread_modes(modes_ref, levels, True)
    build_table(table, False)
    greet((("space", sources),))
    loads[0].wait()
    for k in range(members):
        loads[k + 1].wait()

        @pl.loop(0, groups * (NLON // width))
        def _(i):
            g, c = i // (NLON // width), lax.rem(i, NLON // width)
            rows = pl.ds(pl.multiple_of(g * TILE, TILE), TILE)
            columns = pl.ds(pl.multiple_of(c * width, width), width)
            product = ens[k, :, rows, columns] * vec[:, rows, columns]
            result = nn(weight_ref[...], product.reshape(levels * TILE, width))
            result = result.astype(BF16).reshape(2, TILE // 2, NMODE, width)
            for h in range(2):
                fields[pl.ds(g * (TILE // 2), TILE // 2), h, k, :, columns] = result[h]

    lat_width = groups * members * NMODE
    trade = Exchange(sources, lambda step, i, part: packed.at[step * ROW + i], lambda source, part: out_ref.at[source], *sems)
    for step in STEPS:
        lhs = jnp.concatenate(
            [table[pl.ds(pl.multiple_of(trade.device(step, i) * share, share), share), :] for i in range(ROW)], axis=0
        )
        for pair in range(TILE // 2):
            rhs = fields[2 * pair : 2 * pair + 2].reshape(2 * lat_width, NLON)
            result = nt(lhs, rhs)
            turn[:, 2 * pair, :] = result[:, :LANES]
            turn[:, 2 * pair + 1, :] = result[:, LANES:]
        for i in range(ROW):
            packed[step * ROW + i] = turn[i * share : (i + 1) * share].astype(BF16)
        trade.start(step, 0)
    trade.finish(0)


def inverse_kernel(sources, arrived, legendre, factor, ens_hbm, modes_ref, out_ref,
                   landing, packed, lift_ref, ens, table, turn, turned, fields, mine, theirs,
                   load_sem, mem_send, mem_recv, *sems):
    own_waves = legendre.shape[0]
    members, levels, lat_rows = ens.shape[:3]
    groups = lat_rows // TILE
    eight = TILE // 2
    half = LANES // 2
    middle = own_waves // 2
    width = mine.shape[2]
    pieces = NLON // width
    load = pltpu.make_async_copy(ens_hbm, ens, load_sem.at[0])
    load.start()

    trade = Exchange(
        sources,
        lambda step, i, part: packed.at[trade.device(step, i), part // 2, pl.ds(part % 2 * middle, middle)],
        lambda source, part: landing.at[source, part // 2, pl.ds(part % 2 * middle, middle)],
        *sems,
    )
    other = 1 - lax.axis_index("mem")
    greet((("space", sources), ("mem", 2)))

    def wave(m):
        rows = legendre[m].astype(F32).reshape(sources * groups, 2, eight, NDEG)
        halves = [rows[:, h].reshape(sources * TILE, NDEG).astype(BF16) for h in range(2)]
        stacked = [arrived[:, 2 * m + r].reshape(sources * TILE, LANES).T for r in range(2)]
        harmonic = 0.0
        for h in range(2):
            lhs = jnp.concatenate([z[h * half : (h + 1) * half] for z in stacked], axis=0)
            harmonic = harmonic + nn(lhs, halves[h])
        weighted = (harmonic * factor[pl.ds(m, 1), :]).astype(BF16)
        zero = jnp.zeros((half, NDEG), BF16)
        low = jnp.concatenate([weighted[:half], zero, weighted[half:], zero], axis=0)
        high = jnp.concatenate([zero, weighted[:half], zero, weighted[half:]], axis=0)
        synthesis = nt(halves[0], low) + nt(halves[1], high)
        parts = [synthesis[:, r * LANES : (r + 1) * LANES].reshape(sources, groups, eight, LANES) for r in range(2)]
        packed[:, :, m] = jnp.concatenate(parts, axis=2).astype(BF16)

    pl.loop(0, middle)(wave)
    for step in STEPS:
        trade.start(step, 0)
    pl.loop(middle, own_waves)(wave)
    for part in (1, 2, 3):
        for step in STEPS:
            trade.start(step, part)
    lift_ref[...] = spread_modes(modes_ref, levels, False)
    build_table(table, True)
    load.wait()
    for g in range(groups):
        trade.finish(2 * g)
        trade.finish(2 * g + 1)

        @pl.loop(0, sources)
        def _(source):
            turn[pl.ds(pl.multiple_of(source * own_waves, own_waves), own_waves)] = landing[source, g].astype(F32)

        for t in range(eight):
            column = jnp.concatenate([turn[:, r * eight + t, :] for r in range(2)], axis=0)
            turned[t] = column.astype(BF16).T

        @pl.loop(0, pieces)
        def _(c):
            columns = pl.ds(pl.multiple_of(c * width, width), width)
            for quad in range(eight // 4):
                lhs = turned[4 * quad : 4 * quad + 4].reshape(4 * LANES, 2 * M)
                result = nn(lhs, table[:, columns]).astype(BF16).reshape(4, 2, members, NMODE, width)
                for i in range(4):
                    for h in range(2):
                        fields[:, h * eight + 4 * quad + i] = result[i, h]
            total = 0.0
            for k in range(members):
                lifted = nn(lift_ref[...], fields[k].reshape(TILE * NMODE, width))
                anomaly = ens[k, :, g * TILE : (g + 1) * TILE, columns].reshape(levels * TILE, width)
                total = total + lifted * anomaly.astype(F32)
            at = g * pieces + c
            mine[at] = total.astype(BF16)
            send("mem", mine.at[at], theirs.at[at], mem_send.at[at], mem_recv.at[at], other).start()

    scale = 1.0 / (2 * members - 1)
    for g in range(groups):

        @pl.loop(0, pieces)
        def _(c):
            at = g * pieces + c
            columns = pl.ds(pl.multiple_of(c * width, width), width)
            send("mem", mine.at[at], theirs.at[at], mem_send.at[at], mem_recv.at[at], other).wait()
            summed = (mine[at].astype(F32) + theirs[at].astype(F32)) * scale
            out_ref[:, g * TILE : (g + 1) * TILE, columns] = summed.astype(BF16).reshape(levels, TILE, width)


def params(number):
    return pltpu.CompilerParams(collective_id=number, has_side_effects=True, vmem_limit_bytes=BIG)


def kernel_path(ensemble, vector, modes, legendre, spectrum, truncation):
    members, levels, lat_rows, _ = ensemble.shape
    own_waves = legendre.shape[0]
    sources = lax.axis_size("space")
    share = 2 * own_waves
    narrow = modes.astype(BF16)
    wavenumber = (
        lax.axis_index("space") * own_waves
        + jnp.arange(own_waves, dtype=jnp.int32)[:, None]
        + jnp.arange(NDEG, dtype=jnp.int32)[None, :]
    )
    factor = jnp.where(wavenumber <= truncation[0], spectrum, jnp.zeros_like(spectrum))
    any_space = pl.BlockSpec(memory_space=pl.ANY)
    vmem = pl.BlockSpec(memory_space=pltpu.VMEM)
    exchanged = jax.ShapeDtypeStruct((sources, share, TILE, LANES), BF16)
    groups = lat_rows // TILE
    width = 256
    pieces = groups * (NLON // width)
    dma = pltpu.SemaphoreType.DMA
    arrived = pl.pallas_call(
        lambda *refs: forward_kernel(sources, *refs),
        out_shape=exchanged,
        in_specs=[any_space, any_space, vmem],
        out_specs=any_space,
        scratch_shapes=[
            pltpu.VMEM((TILE * NMODE, levels * TILE), BF16),
            pltpu.VMEM(ensemble.shape, BF16),
            pltpu.VMEM(vector.shape, BF16),
            pltpu.VMEM((2 * M, NLON), BF16),
            pltpu.VMEM((TILE, 2, members, NMODE, NLON), BF16),
            pltpu.VMEM((4 * share, TILE, LANES), F32),
            pltpu.VMEM((sources, share, TILE, LANES), BF16),
            dma((members + 1,)),
            dma((1,)),
            dma((1, sources)),
            dma((1, sources)),
        ],
        compiler_params=params(0),
        name="forward",
    )(ensemble, vector, narrow)
    traded = pltpu.VMEM((sources, groups, own_waves, TILE, LANES), BF16)
    parts = 2 * groups
    return pl.pallas_call(
        lambda *refs: inverse_kernel(sources, *refs),
        out_shape=jax.ShapeDtypeStruct(vector.shape, BF16),
        in_specs=[vmem, vmem, vmem, any_space, vmem],
        out_specs=vmem,
        scratch_shapes=[
            traded,
            traded,
            pltpu.VMEM((levels * TILE, TILE * NMODE), BF16),
            pltpu.VMEM(ensemble.shape, BF16),
            pltpu.VMEM((2 * M, NLON), BF16),
            pltpu.VMEM((M, TILE, LANES), F32),
            pltpu.VMEM((TILE // 2, LANES, 2 * M), BF16),
            pltpu.VMEM((members, TILE, NMODE, width), BF16),
            pltpu.VMEM((pieces, levels * TILE, width), BF16),
            pltpu.VMEM((pieces, levels * TILE, width), BF16),
            dma((1,)),
            dma((pieces,)),
            dma((pieces,)),
            dma((parts,)),
            dma((parts, sources)),
            dma((parts, sources)),
        ],
        compiler_params=params(1),
        name="inverse",
    )(arrived, legendre, factor, ensemble, narrow)


def on_device(ensemble, vector, modes, legendre, spectrum, truncation):
    fits = (
        lax.axis_size("mem") == 2
        and lax.axis_size("space") == 4 * ROW
        and ensemble.shape[2] == 2 * TILE
        and 2 * ensemble.shape[0] * NMODE == LANES
        and modes.shape[1] == 32
    )
    path = kernel_path if fits else plain_path
    return path(ensemble, vector, modes, legendre, spectrum, truncation)


def solution(mesh):
    placed = (
        P("mem", None, "space", None),
        P(None, "space", None),
        P(),
        P("space", None, None),
        P("space", None),
        P(),
    )
    return jax.shard_map(
        on_device, mesh=mesh, in_specs=placed, out_specs=P(None, "space", None), check_vma=False
    )
```

```python
import math

import jax
import jax.numpy as jnp
from jax import lax
from jax.experimental import pallas as pl
from jax.experimental.pallas import tpu as pltpu
from jax.sharding import PartitionSpec as P

NMODE = 16
NLON = 1536
M = 512
NDEG = 256


def fourier_table(length, wave_count):
    points = jnp.arange(length, dtype=jnp.int32)
    orders = jnp.arange(wave_count, dtype=jnp.int32)
    phases = points[:, None] * orders[None, :] % length
    angles = phases.astype(jnp.float32) * (2.0 * math.pi / length)
    amplitude = math.sqrt(2.0 / length)
    stacked = jnp.stack([jnp.cos(angles), -jnp.sin(angles)], axis=-1) * amplitude
    return stacked.reshape(length, 2 * wave_count).astype(jnp.bfloat16)


def plain_path(ensemble, vector, modes, legendre, spectrum, truncation):
    members = ensemble.shape[0]
    lat_rows = ensemble.shape[2]
    own_waves = legendre.shape[0]
    sources = lax.axis_size("space")
    total_members = members * lax.axis_size("mem")
    highest = lax.Precision.HIGHEST
    fourier = fourier_table(NLON, M)
    product = ensemble.astype(jnp.float32) * vector.astype(jnp.float32)[None]
    projected = jnp.einsum("jl,klac->kjac", modes, product, precision=highest).astype(jnp.bfloat16)
    fields = members * NMODE
    columns = fields * lat_rows
    zonal_parts = lax.dot_general(
        fourier,
        projected.reshape(columns, NLON),
        (((0,), (1,)), ((), ())),
        preferred_element_type=jnp.float32,
    )
    zonal_parts = zonal_parts.astype(jnp.bfloat16).reshape(1, 2 * M, columns)
    first_wave = lax.axis_index("space") * own_waves
    wavenumber = (
        first_wave
        + jnp.arange(own_waves, dtype=jnp.int32)[:, None]
        + jnp.arange(NDEG, dtype=jnp.int32)[None, :]
    )
    factor = jnp.where(wavenumber <= truncation[0], spectrum, jnp.zeros_like(spectrum))
    arrived = lax.all_to_all(zonal_parts, "space", split_axis=1, concat_axis=0, tiled=True)
    arrived = arrived.reshape(sources, own_waves, 2, fields, lat_rows)
    legendre_view = legendre.reshape(own_waves, sources, lat_rows, NDEG)
    harmonic = jnp.einsum(
        "smrfa,msan->mrfn", arrived, legendre_view, preferred_element_type=jnp.float32
    )
    weighted = (harmonic * factor[:, None, None, :]).astype(jnp.bfloat16)
    synthesis = jnp.einsum(
        "mrfn,msan->smrfa", weighted, legendre_view, preferred_element_type=jnp.float32
    )
    synthesis = synthesis.astype(jnp.bfloat16).reshape(sources, 2 * own_waves, columns)
    returned = lax.all_to_all(synthesis, "space", split_axis=0, concat_axis=1, tiled=True)
    spread = lax.dot_general(
        returned.reshape(2 * M, columns),
        fourier,
        (((0,), (1,)), ((), ())),
        preferred_element_type=jnp.float32,
    )
    spread = spread.reshape(members, NMODE, lat_rows, NLON)
    lifted = jnp.einsum("jl,kjac->klac", modes, spread, precision=highest)
    partial_value = jnp.sum(ensemble.astype(jnp.float32) * lifted, axis=0)
    summed = lax.psum(partial_value.astype(jnp.bfloat16), "mem").astype(jnp.float32)
    return (summed / (total_members - 1)).astype(jnp.bfloat16)


F32 = jnp.float32
BF16 = jnp.bfloat16
TILE = 16
LANES = 128
BIG = 63 * 1024 * 1024


def nt(a, b):
    return lax.dot_general(a, b, (((1,), (1,)), ((), ())), preferred_element_type=F32)


def nn(a, b):
    return lax.dot_general(a, b, (((1,), (0,)), ((), ())), preferred_element_type=F32)


def cosine(phase):
    phase = lax.rem(phase, NLON)
    offset = (jnp.abs(phase - NLON // 2) - NLON // 4).astype(F32)
    x = offset * (2.0 * math.pi / NLON)
    square = x * x
    value = 1.0
    for n in range(6, 0, -1):
        value = 1.0 - square * value * (1.0 / ((2 * n) * (2 * n + 1)))
    return x * value


def build_table(table_ref, waves_first):
    rows = 128
    quarter = NLON // 4
    amplitude = math.sqrt(2.0 / NLON)

    @pl.loop(0, 2 * M // rows)
    def _(i):
        start = pl.multiple_of(i * rows, rows)
        row = start + lax.broadcasted_iota(jnp.int32, (rows, LANES), 0)
        lane = lax.broadcasted_iota(jnp.int32, (rows, LANES), 1)
        wave, part = (lax.rem(row, M), row // M) if waves_first else (row // 2, lax.rem(row, 2))
        low_cos = cosine(wave * lane)
        low_sin = cosine(wave * lane + 3 * quarter)
        high = cosine(wave * LANES * lax.rem(lane, 64) + (part + 3 * (lane // 64)) * quarter) * amplitude
        for c in range(NLON // LANES):
            value = high[:, c : c + 1] * low_cos - high[:, 64 + c : 65 + c] * low_sin
            table_ref[pl.ds(start, rows), c * LANES : (c + 1) * LANES] = value.astype(BF16)


def greet(counts):
    barrier = pltpu.get_barrier_semaphore()
    for axis, count in counts:
        me = lax.axis_index(axis)
        for i in range(1, count):
            target = lax.rem(me + i, count)
            pl.semaphore_signal(barrier, inc=1, device_id={axis: target}, device_id_type=pl.DeviceIdType.MESH)
    pl.semaphore_wait(barrier, sum(count - 1 for _, count in counts))


def send(axis, src, dst, send_sem, recv_sem, target):
    return pltpu.make_async_remote_copy(
        src_ref=src,
        dst_ref=dst,
        send_sem=send_sem,
        recv_sem=recv_sem,
        device_id={axis: target},
        device_id_type=pl.DeviceIdType.MESH,
    )


def spread_modes(modes_ref, levels, across):
    tiled = jnp.concatenate([modes_ref[...].astype(BF16)] * TILE, axis=0)
    long, short = levels * TILE, TILE * NMODE
    if across:
        pick = (lax.broadcasted_iota(jnp.int32, (levels, long), 1) // TILE) == lax.broadcasted_iota(jnp.int32, (levels, long), 0)
        value = nn(tiled, jnp.where(pick, 1.0, 0.0).astype(BF16))
        shape, long_at = (short, long), 1
    else:
        pick = (lax.broadcasted_iota(jnp.int32, (long, levels), 0) // TILE) == lax.broadcasted_iota(jnp.int32, (long, levels), 1)
        value = nt(jnp.where(pick, 1.0, 0.0).astype(BF16), tiled)
        shape, long_at = (long, short), 0
    agree = (lax.broadcasted_iota(jnp.int32, shape, long_at) % TILE) == (lax.broadcasted_iota(jnp.int32, shape, 1 - long_at) // NMODE)
    return jnp.where(agree, value, 0.0).astype(BF16)


ROW = 4
QUARTERS = 4
STEPS = (2, 1, 3, 0)


class Exchange:
    def __init__(self, sources, sources_at, landing_at, own_sem, send_sem, recv_sem):
        self.count = sources // ROW
        self.me = lax.axis_index("space")
        self.row, self.column = self.me // ROW, lax.rem(self.me, ROW)
        self.sources_at, self.landing_at = sources_at, landing_at
        self.own_sem, self.send_sem, self.recv_sem = own_sem, send_sem, recv_sem

    def device(self, step, i):
        return lax.rem(self.row + step + self.count, self.count) * ROW + lax.rem(self.column + i + ROW, ROW)

    def piece(self, step, i, part, source):
        at = step * ROW + i
        return send("space", self.sources_at(step, i, part), self.landing_at(source, part),
                    self.send_sem.at[part, at], self.recv_sem.at[part, at], self.device(step, i))

    def own(self, part):
        return pltpu.make_async_copy(self.sources_at(0, 0, part), self.landing_at(self.me, part), self.own_sem.at[part])

    def start(self, step, part):
        for i in range(ROW):
            if step == 0 and i == 0:
                self.own(part).start()
            else:
                self.piece(step, i, part, self.me).start()

    def finish(self, part):
        for step in STEPS:
            for i in range(ROW):
                if step == 0 and i == 0:
                    self.own(part).wait()
                else:
                    self.piece(step, i, part, self.device(-step, -i)).wait()


def forward_kernel(sources, ens_hbm, vec_hbm, modes_ref, out_ref,
                   weight_ref, ens, vec, table, fields, turn, packed, load_sem, *sems):
    me = lax.axis_index("space")
    members = ens.shape[0]
    groups = ens.shape[2] // TILE
    share = 2 * M // sources
    width = 512
    loads = [pltpu.make_async_copy(vec_hbm, vec, load_sem.at[members])]
    loads += [pltpu.make_async_copy(ens_hbm.at[k], ens.at[k], load_sem.at[k]) for k in range(members)]
    for load in loads:
        load.start()
    levels = ens.shape[1]
    weight_ref[...] = spread_modes(modes_ref, levels, True)
    build_table(table, False)
    greet((("space", sources),))
    loads[0].wait()
    for k in range(members):
        loads[k + 1].wait()

        @pl.loop(0, groups * (NLON // width))
        def _(i):
            g, c = i // (NLON // width), lax.rem(i, NLON // width)
            rows = pl.ds(pl.multiple_of(g * TILE, TILE), TILE)
            columns = pl.ds(pl.multiple_of(c * width, width), width)
            product = ens[k, :, rows, columns] * vec[:, rows, columns]
            result = nn(weight_ref[...], product.reshape(levels * TILE, width))
            result = result.astype(BF16).reshape(2, TILE // 2, NMODE, width)
            for h in range(2):
                fields[pl.ds(g * (TILE // 2), TILE // 2), h, k, :, columns] = result[h]

    lat_width = groups * members * NMODE
    trade = Exchange(sources, lambda step, i, part: packed.at[step * ROW + i], lambda source, part: out_ref.at[source], *sems)
    for step in STEPS:
        lhs = jnp.concatenate(
            [table[pl.ds(pl.multiple_of(trade.device(step, i) * share, share), share), :] for i in range(ROW)], axis=0
        )
        for pair in range(TILE // 2):
            rhs = fields[2 * pair : 2 * pair + 2].reshape(2 * lat_width, NLON)
            result = nt(lhs, rhs)
            turn[:, 2 * pair, :] = result[:, :LANES]
            turn[:, 2 * pair + 1, :] = result[:, LANES:]
        for i in range(ROW):
            packed[step * ROW + i] = turn[i * share : (i + 1) * share].astype(BF16)
        trade.start(step, 0)
    trade.finish(0)


def inverse_kernel(sources, arrived_hbm, legendre_hbm, factor, ens_hbm, modes_ref, out_ref,
                   arrived, legendre, landing, packed, lift_ref, ens, table, turn, turned, fields, mine, theirs,
                   load_sem, first_sem, mem_send, mem_recv, *sems):
    own_waves = legendre.shape[0]
    members, levels, lat_rows = ens.shape[:3]
    groups = lat_rows // TILE
    eight = TILE // 2
    half = LANES // 2
    few = own_waves // QUARTERS
    width = mine.shape[2]
    pieces = NLON // width
    load = pltpu.make_async_copy(ens_hbm, ens, load_sem.at[0])
    firsts = []
    for q in range(QUARTERS):
        own, pair = pl.ds(q * few, few), pl.ds(2 * q * few, 2 * few)
        firsts.append((
            pltpu.make_async_copy(arrived_hbm.at[:, pair], arrived.at[:, pair], first_sem.at[0, q]),
            pltpu.make_async_copy(legendre_hbm.at[own], legendre.at[own], first_sem.at[1, q]),
        ))
        for first in firsts[q]:
            first.start()
    load.start()

    trade = Exchange(
        sources,
        lambda step, i, part: packed.at[trade.device(step, i), part // QUARTERS, pl.ds(part % QUARTERS * few, few)],
        lambda source, part: landing.at[source, part // QUARTERS, pl.ds(part % QUARTERS * few, few)],
        *sems,
    )
    other = 1 - lax.axis_index("mem")
    greet((("space", sources), ("mem", 2)))

    def wave(m):
        rows = legendre[m].astype(F32).reshape(sources * groups, 2, eight, NDEG)
        halves = [rows[:, h].reshape(sources * TILE, NDEG).astype(BF16) for h in range(2)]
        stacked = [arrived[:, 2 * m + r].reshape(sources * TILE, LANES).T for r in range(2)]
        harmonic = 0.0
        for h in range(2):
            lhs = jnp.concatenate([z[h * half : (h + 1) * half] for z in stacked], axis=0)
            harmonic = harmonic + nn(lhs, halves[h])
        weighted = (harmonic * factor[pl.ds(m, 1), :]).astype(BF16)
        zero = jnp.zeros((half, NDEG), BF16)
        low = jnp.concatenate([weighted[:half], zero, weighted[half:], zero], axis=0)
        high = jnp.concatenate([zero, weighted[:half], zero, weighted[half:]], axis=0)
        synthesis = nt(halves[0], low) + nt(halves[1], high)
        parts = [synthesis[:, r * LANES : (r + 1) * LANES].reshape(sources, groups, eight, LANES) for r in range(2)]
        packed[:, :, m] = jnp.concatenate(parts, axis=2).astype(BF16)

    for q in range(QUARTERS):
        for first in firsts[q]:
            first.wait()
        pl.loop(q * few, (q + 1) * few)(wave)
        for step in STEPS:
            trade.start(step, q)
    for part in range(QUARTERS, groups * QUARTERS):
        for step in STEPS:
            trade.start(step, part)
    lift_ref[...] = spread_modes(modes_ref, levels, False)
    build_table(table, True)
    load.wait()
    for g in range(groups):
        for q in range(QUARTERS):
            trade.finish(g * QUARTERS + q)

        @pl.loop(0, sources)
        def _(source):
            turn[pl.ds(pl.multiple_of(source * own_waves, own_waves), own_waves)] = landing[source, g].astype(F32)

        for t in range(eight):
            column = jnp.concatenate([turn[:, r * eight + t, :] for r in range(2)], axis=0)
            turned[t] = column.astype(BF16).T

        @pl.loop(0, pieces)
        def _(c):
            columns = pl.ds(pl.multiple_of(c * width, width), width)
            for quad in range(eight // 4):
                lhs = turned[4 * quad : 4 * quad + 4].reshape(4 * LANES, 2 * M)
                result = nn(lhs, table[:, columns]).astype(BF16).reshape(4, 2, members, NMODE, width)
                for i in range(4):
                    for h in range(2):
                        fields[:, h * eight + 4 * quad + i] = result[i, h]
            total = 0.0
            for k in range(members):
                lifted = nn(lift_ref[...], fields[k].reshape(TILE * NMODE, width))
                anomaly = ens[k, :, g * TILE : (g + 1) * TILE, columns].reshape(levels * TILE, width)
                total = total + lifted * anomaly.astype(F32)
            at = g * pieces + c
            mine[at] = total.astype(BF16)
            send("mem", mine.at[at], theirs.at[at], mem_send.at[at], mem_recv.at[at], other).start()

    scale = 1.0 / (2 * members - 1)
    for g in range(groups):

        @pl.loop(0, pieces)
        def _(c):
            at = g * pieces + c
            columns = pl.ds(pl.multiple_of(c * width, width), width)
            send("mem", mine.at[at], theirs.at[at], mem_send.at[at], mem_recv.at[at], other).wait()
            summed = (mine[at].astype(F32) + theirs[at].astype(F32)) * scale
            out_ref[:, g * TILE : (g + 1) * TILE, columns] = summed.astype(BF16).reshape(levels, TILE, width)


def params(number):
    return pltpu.CompilerParams(collective_id=number, has_side_effects=True, vmem_limit_bytes=BIG)


def kernel_path(ensemble, vector, modes, legendre, spectrum, truncation):
    members, levels, lat_rows, _ = ensemble.shape
    own_waves = legendre.shape[0]
    sources = lax.axis_size("space")
    share = 2 * own_waves
    wavenumber = (
        lax.axis_index("space") * own_waves
        + jnp.arange(own_waves, dtype=jnp.int32)[:, None]
        + jnp.arange(NDEG, dtype=jnp.int32)[None, :]
    )
    factor = jnp.where(wavenumber <= truncation[0], spectrum, jnp.zeros_like(spectrum))
    any_space = pl.BlockSpec(memory_space=pl.ANY)
    vmem = pl.BlockSpec(memory_space=pltpu.VMEM)
    exchanged = jax.ShapeDtypeStruct((sources, share, TILE, LANES), BF16)
    groups = lat_rows // TILE
    width = 256
    pieces = groups * (NLON // width)
    dma = pltpu.SemaphoreType.DMA
    arrived = pl.pallas_call(
        lambda *refs: forward_kernel(sources, *refs),
        out_shape=exchanged,
        in_specs=[any_space, any_space, vmem],
        out_specs=any_space,
        scratch_shapes=[
            pltpu.VMEM((TILE * NMODE, levels * TILE), BF16),
            pltpu.VMEM(ensemble.shape, BF16),
            pltpu.VMEM(vector.shape, BF16),
            pltpu.VMEM((2 * M, NLON), BF16),
            pltpu.VMEM((TILE, 2, members, NMODE, NLON), BF16),
            pltpu.VMEM((4 * share, TILE, LANES), F32),
            pltpu.VMEM((sources, share, TILE, LANES), BF16),
            dma((members + 1,)),
            dma((1,)),
            dma((1, sources)),
            dma((1, sources)),
        ],
        compiler_params=params(0),
        name="forward",
    )(ensemble, vector, modes)
    traded = pltpu.VMEM((sources, groups, own_waves, TILE, LANES), BF16)
    parts = QUARTERS * groups
    return pl.pallas_call(
        lambda *refs: inverse_kernel(sources, *refs),
        out_shape=jax.ShapeDtypeStruct(vector.shape, BF16),
        in_specs=[any_space, any_space, vmem, any_space, vmem],
        out_specs=vmem,
        scratch_shapes=[
            pltpu.VMEM(exchanged.shape, BF16),
            pltpu.VMEM(legendre.shape, BF16),
            traded,
            traded,
            pltpu.VMEM((levels * TILE, TILE * NMODE), BF16),
            pltpu.VMEM(ensemble.shape, BF16),
            pltpu.VMEM((2 * M, NLON), BF16),
            pltpu.VMEM((M, TILE, LANES), F32),
            pltpu.VMEM((TILE // 2, LANES, 2 * M), BF16),
            pltpu.VMEM((members, TILE, NMODE, width), BF16),
            pltpu.VMEM((pieces, levels * TILE, width), BF16),
            pltpu.VMEM((pieces, levels * TILE, width), BF16),
            dma((1,)),
            dma((2, QUARTERS)),
            dma((pieces,)),
            dma((pieces,)),
            dma((parts,)),
            dma((parts, sources)),
            dma((parts, sources)),
        ],
        compiler_params=params(1),
        name="inverse",
    )(arrived, legendre, factor, ensemble, modes)


def on_device(ensemble, vector, modes, legendre, spectrum, truncation):
    fits = (
        lax.axis_size("mem") == 2
        and lax.axis_size("space") == 4 * ROW
        and ensemble.shape[2] == 2 * TILE
        and 2 * ensemble.shape[0] * NMODE == LANES
        and modes.shape[1] == 32
    )
    path = kernel_path if fits else plain_path
    return path(ensemble, vector, modes, legendre, spectrum, truncation)


def solution(mesh):
    placed = (
        P("mem", None, "space", None),
        P(None, "space", None),
        P(),
        P("space", None, None),
        P("space", None),
        P(),
    )
    return jax.shard_map(
        on_device, mesh=mesh, in_specs=placed, out_specs=P(None, "space", None), check_vma=False
    )
```
